1024 devices in a mesh: dp: 32 (over x_lo, z), seq: 32 (over y, x_hi, core).
Axes of the slice: x: 4 (x_hi: 2, x_lo: 2; x = x_hi * 2 + x_lo), y: 8, z: 16, core: 2. Of those that a mesh axis runs over, the one named last changes fastest.
Arguments:
- q_raw: bfloat16 [32, 4096, 2048], P('dp', 'seq'), may hold values from -500 to 500
- key_projection: bfloat16 [32, 4096, 1024], P('dp', 'seq'), may hold values from -500 to 500
- values: bfloat16 [32, 4096, 1024], P('dp', 'seq'), may hold values from -6 to 6
- output_gradient: bfloat16 [32, 4096, 2048], P('dp', 'seq'), may hold values from -20 to 20
- q_gain: float32 [128], replicated, may hold values from 0.5 to 6
- key_norm_gain: float32 [128], replicated, may hold values from 0.5 to 6
- lengths: int32 [32, 16], P('dp'), may hold values from 1 to 1024, 4096 in all within a row
Outputs:
- q_raw_grad: bfloat16 [32, 4096, 2048], P('dp', 'seq')
- k_raw_grad: bfloat16 [32, 4096, 1024], P('dp', 'seq')
- values_grad: bfloat16 [32, 4096, 1024], P('dp', 'seq')
- q_gain_grad: float32 [128], replicated
- key_gain_gradient: float32 [128], replicated
The draws below stay inside these ranges and needn't reach their ends.
Inputs may be any that keep to these rules, and one draw needn't show every extreme that they name: Each row's 16 lengths sum to 4096; the longest of a row is 1024.
All inputs are finite; a program needn't handle non-finite values.
Results may differ from the reference program's by a relative error of at most 0.04.
The reference program's roundings to bfloat16 on the way count: a program that leaves them out, or rounds other values in their place, can miss the bound.
Values may be sent and summed in bfloat16 or wider, within the bound.
No kernel may reach another device: no remote copies, remote signals or barrier semaphores. Data moves between devices by JAX's collectives and lax.ppermute only.
A program may use at most 32 MiB of HBM per device.

```python
import math
import jax
import jax.numpy as jnp
import numpy as np
from jax import lax

QUERY_HEADS = 16
KEY_VALUE_HEADS = 8
HEAD_SIZE = 128
WINDOW = 256
REACH = 2
NDOC = 16
TOK_DEV = 128
ROW_LENGTH = 4096
PACKED_ROWS = 32


def broadcast_heads(sub_key, dims_shape):
    return jnp.exp(jax.random.uniform(sub_key, dims_shape, jnp.float32, math.log(0.5), math.log(5.0)))


def shared_fields(base_key):
    random_subkeys = jax.random.split(jax.random.fold_in(base_key, 7), 6)
    query_shape = (PACKED_ROWS, ROW_LENGTH, QUERY_HEADS, HEAD_SIZE)
    key_dimensions = (PACKED_ROWS, ROW_LENGTH, KEY_VALUE_HEADS, HEAD_SIZE)
    query_base = jnp.clip(jax.random.normal(random_subkeys[0], query_shape, jnp.float32), -6.0, 6.0)
    key_offset_start = jnp.clip(jax.random.normal(random_subkeys[1], key_dimensions, jnp.float32), -6.0, 6.0)
    query_field = query_base * broadcast_heads(random_subkeys[2], (PACKED_ROWS, ROW_LENGTH, QUERY_HEADS, 1)) * broadcast_heads(random_subkeys[3], (QUERY_HEADS, HEAD_SIZE))
    key_layout = key_offset_start * broadcast_heads(random_subkeys[4], (PACKED_ROWS, ROW_LENGTH, KEY_VALUE_HEADS, 1)) * broadcast_heads(random_subkeys[5], (KEY_VALUE_HEADS, HEAD_SIZE))
    query_field = jnp.clip(query_field, -500.0, 500.0).reshape(PACKED_ROWS, ROW_LENGTH, QUERY_HEADS * HEAD_SIZE)
    key_layout = jnp.clip(key_layout, -500.0, 500.0).reshape(PACKED_ROWS, ROW_LENGTH, KEY_VALUE_HEADS * HEAD_SIZE)
    return (query_field, key_layout)


def draw_q_raw(key, part):
    return shared_fields(key)[0].astype(jnp.bfloat16)


def draw_key_projection(key, part):
    return shared_fields(key)[1].astype(jnp.bfloat16)


def draw_output_gradient(key, part):
    random_subkeys = jax.random.split(jax.random.fold_in(key, 17), 1)
    full_shape = (PACKED_ROWS, ROW_LENGTH, QUERY_HEADS * HEAD_SIZE)
    row_rise = 1.0 + 2.0 * jnp.arange(PACKED_ROWS, dtype=jnp.float32) / PACKED_ROWS
    position_rise = 1.0 + 2.0 * jnp.arange(ROW_LENGTH, dtype=jnp.float32) / ROW_LENGTH
    rising = (row_rise[:, None] * position_rise[None, :])[:, :, None] / 3.0
    base_field = jnp.clip(jax.random.normal(random_subkeys[0], full_shape, jnp.float32), -6.0, 6.0)
    return (base_field * rising).astype(jnp.bfloat16)


def gain_field(base_key, salt):
    sub_key = jax.random.fold_in(base_key, salt)
    return jax.random.uniform(sub_key, (HEAD_SIZE,), jnp.float32, 0.5, 2.0)


def draw_q_gain(key, part):
    return gain_field(key, 11)


def draw_key_norm_gain(key, part):
    return gain_field(key, 13)


def shard_levels(key, dims, shards, smallest, high):
    factor_of, own = 1.0, jax.random.fold_in(key, 6)
    for position, shards_of in shards:
        steps = jnp.exp(jax.random.uniform(jax.random.fold_in(own, position), (shards_of,), jnp.float32, smallest / len(shards), high / len(shards)))
        factor_of = factor_of * jnp.repeat(steps, dims[position] // shards_of).reshape([-1 if axis == position else 1 for axis in range(len(dims))])
    return factor_of


def length_profile(number_of, total, limit, skew):
    weights = [(1 << 20) // math.isqrt(rank ** skew) + 1 for rank in range(2, number_of + 1)]
    surplus, counts = total - limit - (number_of - 1), [1] * (number_of - 1)
    while surplus > 0:
        movable = [i for i in range(number_of - 1) if counts[i] < limit]
        pool, left = sum([weights[i] for i in movable]), surplus
        for i in movable:
            addition = min(limit - counts[i], max(1, left * weights[i] // pool), surplus)
            counts[i] = counts[i] + addition
            surplus = surplus - addition
    return np.array([limit] + counts)


def uneven_parts(own_key, number_of, total, reach, skew):
    if number_of == 2:
        one = jax.random.randint(own_key, (), max(1, total - reach), min(reach, total - 1) + 1)
        return jnp.stack([one, total - one])
    sizes = jnp.asarray(length_profile(number_of, total, reach, skew), jnp.int32)
    couples = (number_of - 1) // 2
    giver, sink = sizes[1:1 + 2 * couples:2], sizes[2:2 + 2 * couples:2]
    slack = jnp.minimum(giver - 1, reach - sink)
    passed = jax.random.randint(jax.random.fold_in(own_key, 1), (couples,), 0, 1 << 20) % (slack + 1)
    sizes = sizes.at[1:1 + 2 * couples:2].set(giver - passed).at[2:2 + 2 * couples:2].set(sink + passed)
    return sizes[jax.random.permutation(jax.random.fold_in(own_key, 2), number_of)]


def scatter_about(rng, shape, deviation, bound, cuts=(), held_as=jnp.bfloat16):
    level = shard_levels(rng, shape, cuts, -0.22, 0.18) if cuts else 1.0
    values = jax.random.normal(rng, shape, jnp.float32) * deviation * level
    return jnp.minimum(jnp.maximum(values, -bound), bound).astype(held_as)


def setup_inputs(seed: int = 0) -> dict:
    seeds = jax.random.split(jax.random.key(seed), 8)
    q_raw = draw_q_raw(jax.random.fold_in(seeds[7], 71), 0)
    key_projection = draw_key_projection(jax.random.fold_in(seeds[7], 71), 0)
    values = scatter_about(seeds[2], (PACKED_ROWS, ROW_LENGTH, KEY_VALUE_HEADS * HEAD_SIZE), 1.0, 6.0, ((0, 32), (1, 32)))
    output_gradient = draw_output_gradient(jax.random.fold_in(seeds[7], 71), 0)
    q_gain = draw_q_gain(jax.random.fold_in(seeds[7], 71), 0)
    key_norm_gain = draw_key_norm_gain(jax.random.fold_in(seeds[7], 71), 0)
    lengths = jax.vmap(lambda own: uneven_parts(own, NDOC, ROW_LENGTH, ROW_LENGTH // 4, 2))(jax.random.split(seeds[6], PACKED_ROWS)).reshape((PACKED_ROWS, NDOC)).astype(jnp.int32)
    return {"q_raw": q_raw, "key_projection": key_projection, "values": values, "output_gradient": output_gradient, "q_gain": q_gain, "key_norm_gain": key_norm_gain, "lengths": lengths}


score_scale = 168.0 ** (-0.5)
norm_eps = 1e-06

def apply_norm(raw, gain, heads):
    raw_values = raw.astype(jnp.float32).reshape(raw.shape[:-1] + (heads, HEAD_SIZE))
    inverse = lax.rsqrt(lax.optimization_barrier(jnp.mean(raw_values * raw_values, axis=-1, keepdims=True)) + norm_eps)
    return (raw_values, inverse, (raw_values * inverse * gain).astype(jnp.bfloat16))

def norm_backward(raw_values, inverse, gain, normed_grad):
    scaled = gain * normed_grad
    inner = lax.optimization_barrier(jnp.mean(scaled * raw_values, axis=-1, keepdims=True))
    raw_grad = inverse * scaled - raw_values * inverse * inverse * inverse * inner
    gain_grad = lax.optimization_barrier(jnp.sum((normed_grad * raw_values * inverse).reshape(-1, HEAD_SIZE), axis=0))
    return (raw_grad, gain_grad)

def doc_of(positions, doc_ends):
    return lax.optimization_barrier(jnp.sum((positions[:, None] >= doc_ends[None, :]).astype(jnp.int32), axis=1))

def block_terms(query_block, key_span, value_span, grad_block, block_start, doc_ends):
    key_count = (REACH + 1) * TOK_DEV - 1
    query_pos = block_start + jnp.arange(TOK_DEV, dtype=jnp.int32)
    key_pos = block_start - REACH * TOK_DEV + 1 + jnp.arange(key_count, dtype=jnp.int32)
    query_doc = doc_of(query_pos, doc_ends)
    key_doc = doc_of(key_pos, doc_ends)
    distance = query_pos[:, None] - key_pos[None, :]
    allowed = (query_doc[:, None] == key_doc[None, :]) & (distance >= 0) & (distance < WINDOW) & (key_pos >= 0)[None, :]
    query_f32 = query_block.astype(jnp.float32)
    key_f32 = key_span.astype(jnp.float32)
    value_f32 = value_span.astype(jnp.float32)
    grad_f32 = grad_block.astype(jnp.float32)
    scores = jnp.einsum('qhgd,khd->hgqk', query_f32, key_f32) * score_scale
    scores = jnp.where(allowed[None, None], scores, jnp.float32(-1e+30))
    row_max = lax.optimization_barrier(jnp.max(scores, axis=-1, keepdims=True))
    expanded = jnp.exp(scores - row_max)
    probs = expanded / lax.optimization_barrier(jnp.sum(expanded, axis=-1, keepdims=True))
    probs_low = probs.astype(jnp.bfloat16)
    attended = jnp.einsum('hgqk,khd->qhgd', probs_low.astype(jnp.float32), value_f32).astype(jnp.bfloat16)
    delta_rows = jnp.moveaxis(lax.optimization_barrier(jnp.sum(grad_f32 * attended.astype(jnp.float32), axis=-1)), 0, -1)
    prob_grad = jnp.einsum('qhgd,khd->hgqk', grad_f32, value_f32)
    score_grad = (probs * (prob_grad - delta_rows[..., None])).astype(jnp.bfloat16).astype(jnp.float32)
    query_grad = jnp.einsum('hgqk,khd->qhgd', score_grad, key_f32) * score_scale
    key_grad = jnp.einsum('hgqk,qhgd->khd', score_grad, query_f32) * score_scale
    value_gradient = jnp.einsum('hgqk,qhgd->khd', probs_low.astype(jnp.float32), grad_f32)
    return (query_grad, key_grad, value_gradient)

def split_round(part):
    outside = lax.optimization_barrier(part[:-TOK_DEV].astype(jnp.bfloat16)).astype(jnp.float32)
    return jnp.concatenate([outside, part[-TOK_DEV:]], axis=0)

def reference(q_raw, key_projection, values, output_gradient, q_gain, key_norm_gain, lengths):
    group_count = QUERY_HEADS // KEY_VALUE_HEADS
    block_count = ROW_LENGTH // TOK_DEV
    key_count = (REACH + 1) * TOK_DEV - 1
    padding_rows = REACH * TOK_DEV

    def one_row(item):
        query_row, key_row_slice, value_row_slice, row_gradient, length_row = item
        doc_ends = jnp.cumsum(length_row).astype(jnp.int32)
        query_raw, query_inverse, query_normalized = apply_norm(query_row, q_gain, QUERY_HEADS)
        key_unnormed, key_inverse_norm, key_normalized = apply_norm(key_row_slice, key_norm_gain, KEY_VALUE_HEADS)
        query_head_count = query_normalized.reshape(ROW_LENGTH, KEY_VALUE_HEADS, group_count, HEAD_SIZE)
        head_gradients = row_gradient.reshape(ROW_LENGTH, KEY_VALUE_HEADS, group_count, HEAD_SIZE)
        key_padded = jnp.concatenate([jnp.zeros((padding_rows, KEY_VALUE_HEADS, HEAD_SIZE), jnp.bfloat16), key_normalized.reshape(ROW_LENGTH, KEY_VALUE_HEADS, HEAD_SIZE)], axis=0)
        value_padded = jnp.concatenate([jnp.zeros((padding_rows, KEY_VALUE_HEADS, HEAD_SIZE), jnp.bfloat16), value_row_slice.reshape(ROW_LENGTH, KEY_VALUE_HEADS, HEAD_SIZE)], axis=0)

        def one_block(carry, block):
            key_total, value_total = carry
            start = (block * TOK_DEV).astype(jnp.int32)
            query_block = lax.dynamic_slice_in_dim(query_head_count, start, TOK_DEV, 0)
            grad_block = lax.dynamic_slice_in_dim(head_gradients, start, TOK_DEV, 0)
            key_span = lax.dynamic_slice_in_dim(key_padded, start + 1, key_count, 0)
            value_span = lax.dynamic_slice_in_dim(value_padded, start + 1, key_count, 0)
            query_grad, key_grad, value_gradient = block_terms(query_block, key_span, value_span, grad_block, start, doc_ends)
            key_old = lax.dynamic_slice_in_dim(key_total, start + 1, key_count, 0)
            value_old = lax.dynamic_slice_in_dim(value_total, start + 1, key_count, 0)
            key_total = lax.dynamic_update_slice_in_dim(key_total, key_old + split_round(key_grad), start + 1, 0)
            value_total = lax.dynamic_update_slice_in_dim(value_total, value_old + split_round(value_gradient), start + 1, 0)
            return ((key_total, value_total), query_grad)
        empty_total = jnp.zeros((ROW_LENGTH + padding_rows, KEY_VALUE_HEADS, HEAD_SIZE), jnp.float32)
        (key_total, value_total), query_terms = lax.scan(one_block, (empty_total, empty_total), jnp.arange(block_count, dtype=jnp.int32))
        key_grad = key_total[padding_rows:]
        value_gradient = value_total[padding_rows:]
        query_grad = query_terms.reshape(ROW_LENGTH, QUERY_HEADS, HEAD_SIZE)
        query_unnormed_gradient, query_gain_piece = norm_backward(query_raw, query_inverse, q_gain, query_grad)
        key_unnormed_gradient, key_gain_piece = norm_backward(key_unnormed, key_inverse_norm, key_norm_gain, key_grad)
        return (query_unnormed_gradient.reshape(ROW_LENGTH, QUERY_HEADS * HEAD_SIZE).astype(jnp.bfloat16), key_unnormed_gradient.reshape(ROW_LENGTH, KEY_VALUE_HEADS * HEAD_SIZE).astype(jnp.bfloat16), value_gradient.reshape(ROW_LENGTH, KEY_VALUE_HEADS * HEAD_SIZE).astype(jnp.bfloat16), query_gain_piece, key_gain_piece)
    q_out, k_out, v_out, q_parts, key_pieces = lax.map(one_row, (q_raw, key_projection, values, output_gradient, lengths))
    q_gain_grad = lax.optimization_barrier(jnp.sum(q_parts, axis=0)) / math.sqrt(PACKED_ROWS * ROW_LENGTH * QUERY_HEADS)
    key_gain_gradient = lax.optimization_barrier(jnp.sum(key_pieces, axis=0)) / math.sqrt(PACKED_ROWS * ROW_LENGTH * KEY_VALUE_HEADS)
    return (q_out, k_out, v_out, q_gain_grad, key_gain_gradient)
```

```python
import math

import jax
import jax.numpy as jnp
from jax import lax
from jax.experimental import pallas as pl
from jax.experimental.pallas import tpu as pltpu
from jax.sharding import PartitionSpec as P

QUERY_HEADS = 16
KEY_VALUE_HEADS = 8
HEAD_SIZE = 128
WINDOW = 256
REACH = 2
NDOC = 16

score_scale = 168.0 ** (-0.5)
norm_eps = 1e-06
log2_e = 1.4426950408889634

NT = (((1,), (1,)), ((), ()))
NN = (((1,), (0,)), ((), ()))
TN = (((0,), (0,)), ((), ()))


def shift(block, distance):
    count = lax.axis_size("seq")
    route = [(i, i + distance) for i in range(count) if 0 <= i + distance < count]
    return lax.ppermute(block, "seq", route)


def fold_rows(x):
    return jnp.sum(x.reshape(-1, 8, x.shape[-1]), axis=0)


def attention_kernel(
    start_ref,
    lengths_ref,
    q_ref,
    grad_ref,
    key_ref,
    value_ref,
    near_ref,
    far_ref,
    q_gain_ref,
    key_gain_ref,
    q_out_ref,
    key_own_ref,
    value_own_ref,
    near_out_ref,
    far_out_ref,
    gains_ref,
):
    head = pl.program_id(0)
    tokens = q_ref.shape[0]
    groups = q_ref.shape[1] // HEAD_SIZE
    start = start_ref[0]

    def split(ref):
        whole = ref[...]
        return jnp.concatenate(
            [whole[:, g * HEAD_SIZE : (g + 1) * HEAD_SIZE] for g in range(groups)], axis=0
        )

    q_gain = q_gain_ref[...]
    key_gain = key_gain_ref[...]
    q_raw = split(q_ref).astype(jnp.float32)
    q_inverse = lax.rsqrt(jnp.mean(q_raw * q_raw, axis=-1, keepdims=True) + norm_eps)
    q_unit = q_raw * q_inverse
    q_norm = (q_unit * q_gain).astype(jnp.bfloat16)
    grad = split(grad_ref)
    key_raw = jnp.concatenate([far_ref[0], near_ref[0], key_ref[...]], axis=0).astype(jnp.float32)
    key_inverse = lax.rsqrt(jnp.mean(key_raw * key_raw, axis=-1, keepdims=True) + norm_eps)
    key_unit = key_raw * key_inverse
    key_norm = (key_unit * key_gain).astype(jnp.bfloat16)
    values = jnp.concatenate([far_ref[1], near_ref[1], value_ref[...]], axis=0)

    query_pos = start + lax.broadcasted_iota(jnp.int32, (1, tokens), 1)
    first = jnp.maximum(query_pos - (WINDOW - 1), 0)
    end = jnp.int32(0)
    for c in range(NDOC):
        end = end + lengths_ref[0, c]
        first = jnp.maximum(first, jnp.where(query_pos >= end, end, 0))
    first = jnp.concatenate([first] * groups, axis=1)
    last = jnp.concatenate([query_pos] * groups, axis=1)
    key_pos = (
        start - REACH * tokens + lax.broadcasted_iota(jnp.int32, (3 * tokens, groups * tokens), 0)
    )
    allowed = (key_pos >= first) & (key_pos <= last)

    scores = lax.dot_general(key_norm, q_norm, NT, preferred_element_type=jnp.float32)
    scores = jnp.where(allowed, scores, jnp.float32(-1e30))
    top = jnp.max(scores, axis=0, keepdims=True)
    expanded = jnp.exp2((scores - top) * (score_scale * log2_e))
    probs = expanded * (1.0 / jnp.sum(expanded, axis=0, keepdims=True))
    probs_low = probs.astype(jnp.bfloat16)
    prob_grad = lax.dot_general(values, grad, NT, preferred_element_type=jnp.float32)
    delta = jnp.sum(probs * prob_grad, axis=0, keepdims=True)
    score_grad = (probs * (prob_grad - delta)).astype(jnp.bfloat16)

    value_part = lax.dot_general(probs_low, grad, NN, preferred_element_type=jnp.float32)
    key_part = (
        lax.dot_general(score_grad, q_norm, NN, preferred_element_type=jnp.float32) * score_scale
    )
    q_grad = (
        lax.dot_general(score_grad, key_norm, TN, preferred_element_type=jnp.float32) * score_scale
    )

    scaled = q_gain * q_grad
    inner = jnp.mean(scaled * q_raw, axis=-1, keepdims=True)
    q_out = (
        q_inverse * scaled - q_raw * (q_inverse * q_inverse * q_inverse * inner)
    ).astype(jnp.bfloat16)
    for g in range(groups):
        q_out_ref[:, g * HEAD_SIZE : (g + 1) * HEAD_SIZE] = q_out[g * tokens : (g + 1) * tokens]

    far_key = key_part[:tokens].astype(jnp.bfloat16)
    near_key = key_part[tokens : 2 * tokens].astype(jnp.bfloat16)
    own_key = key_part[2 * tokens :]
    far_out_ref[0] = far_key
    near_out_ref[0] = near_key
    key_own_ref[...] = own_key
    far_out_ref[1] = value_part[:tokens].astype(jnp.bfloat16)
    near_out_ref[1] = value_part[tokens : 2 * tokens].astype(jnp.bfloat16)
    value_own_ref[...] = value_part[2 * tokens :]

    q_piece = fold_rows(q_grad * q_unit)
    key_piece = fold_rows(
        far_key.astype(jnp.float32) * key_unit[:tokens]
        + near_key.astype(jnp.float32) * key_unit[tokens : 2 * tokens]
        + own_key * key_unit[2 * tokens :]
    )
    pieces = jnp.concatenate(
        [
            jnp.sum(q_piece, axis=0, keepdims=True),
            jnp.sum(key_piece, axis=0, keepdims=True),
        ],
        axis=0,
    )

    @pl.when(head == 0)
    def _():
        gains_ref[...] = pieces

    @pl.when(head != 0)
    def _():
        gains_ref[...] += pieces


def finish_kernel(
    key_ref, key_own_ref, value_own_ref, near_ref, far_ref, gain_ref, key_out_ref, value_out_ref
):
    gain = gain_ref[...]
    heads = key_ref.shape[1] // HEAD_SIZE
    for h in range(heads):
        at = slice(h * HEAD_SIZE, (h + 1) * HEAD_SIZE)
        total = (
            key_own_ref[:, at]
            + near_ref[0, :, at].astype(jnp.float32)
            + far_ref[0, :, at].astype(jnp.float32)
        )
        raw = key_ref[:, at].astype(jnp.float32)
        inverse = lax.rsqrt(jnp.mean(raw * raw, axis=-1, keepdims=True) + norm_eps)
        scaled = gain * total
        inner = jnp.mean(scaled * raw, axis=-1, keepdims=True)
        key_out_ref[:, at] = (
            inverse * scaled - raw * (inverse * inverse * inverse * inner)
        ).astype(jnp.bfloat16)
    value_out_ref[...] = (
        value_own_ref[...] + near_ref[1].astype(jnp.float32) + far_ref[1].astype(jnp.float32)
    ).astype(jnp.bfloat16)


def attention(start, lengths, q_raw, grad, key_raw, values, near, far, q_gain, key_gain):
    tokens, key_width = key_raw.shape
    heads = key_width // HEAD_SIZE
    wide = q_raw.shape[1] // heads
    smem = pl.BlockSpec(memory_space=pltpu.SMEM)
    by_head = pl.BlockSpec((tokens, HEAD_SIZE), lambda h: (0, h))
    by_group = pl.BlockSpec((tokens, wide), lambda h: (0, h))
    pair = pl.BlockSpec((2, tokens, HEAD_SIZE), lambda h: (0, 0, h))
    row = pl.BlockSpec((1, HEAD_SIZE), lambda h: (0, 0))
    pair_shape = jax.ShapeDtypeStruct((2, tokens, key_width), jnp.bfloat16)
    own_shape = jax.ShapeDtypeStruct((tokens, key_width), jnp.float32)
    flops = 2 * 5 * 3 * tokens * tokens * q_raw.shape[1]
    return pl.pallas_call(
        attention_kernel,
        grid=(heads,),
        in_specs=[smem, smem, by_group, by_group, by_head, by_head, pair, pair, row, row],
        out_specs=[
            by_group,
            by_head,
            by_head,
            pair,
            pair,
            pl.BlockSpec((2, HEAD_SIZE), lambda h: (0, 0)),
        ],
        out_shape=[
            jax.ShapeDtypeStruct(q_raw.shape, jnp.bfloat16),
            own_shape,
            own_shape,
            pair_shape,
            pair_shape,
            jax.ShapeDtypeStruct((2, HEAD_SIZE), jnp.float32),
        ],
        cost_estimate=pl.CostEstimate(
            flops=flops, bytes_accessed=12 * tokens * q_raw.shape[1], transcendentals=0
        ),
        name="window_attention",
    )(start, lengths, q_raw, grad, key_raw, values, near, far, q_gain, key_gain)


def finish(key_raw, key_own, value_own, near, far, key_gain):
    tokens, key_width = key_raw.shape
    blocks = 4
    wide = key_width // blocks
    flat = pl.BlockSpec((tokens, wide), lambda h: (0, h))
    pair = pl.BlockSpec((2, tokens, wide), lambda h: (0, 0, h))
    row = pl.BlockSpec((1, HEAD_SIZE), lambda h: (0, 0))
    shape = jax.ShapeDtypeStruct((tokens, key_width), jnp.bfloat16)
    return pl.pallas_call(
        finish_kernel,
        grid=(blocks,),
        in_specs=[flat, flat, flat, pair, pair, row],
        out_specs=[flat, flat],
        out_shape=[shape, shape],
        cost_estimate=pl.CostEstimate(
            flops=20 * tokens * key_width,
            bytes_accessed=22 * tokens * key_width,
            transcendentals=0,
        ),
        name="finish_keys",
    )(key_raw, key_own, value_own, near, far, key_gain)


def local(q_raw, key_projection, values, output_gradient, q_gain, key_norm_gain, lengths):
    rows, tokens, query_width = q_raw.shape
    seq_count = lax.axis_size("seq")
    start = (lax.axis_index("seq") * tokens).astype(jnp.int32).reshape(1)
    key_raw, value = key_projection[0], values[0]
    key_gain = key_norm_gain.reshape(1, HEAD_SIZE)

    both = jnp.stack([key_raw, value])
    far = shift(both, 2)
    near = shift(both, 1)
    q_out, key_own, value_own, near_part, far_part, gains = attention(
        start,
        lengths,
        q_raw[0],
        output_gradient[0],
        key_raw,
        value,
        near,
        far,
        q_gain.reshape(1, HEAD_SIZE),
        key_gain,
    )
    far_back = shift(far_part, -2)
    near_back = shift(near_part, -1)
    gains = lax.psum(gains, ("dp", "seq"))
    key_out, value_out = finish(key_raw, key_own, value_own, near_back, far_back, key_gain)
    token_total = rows * lax.axis_size("dp") * tokens * seq_count
    return (
        q_out[None],
        key_out[None],
        value_out[None],
        gains[0] / math.sqrt(token_total * QUERY_HEADS),
        gains[1] / math.sqrt(token_total * KEY_VALUE_HEADS),
    )


def solution(mesh):
    by_token = P("dp", "seq", None)
    in_specs = (by_token, by_token, by_token, by_token, P(), P(), P("dp", None))
    out_specs = (by_token, by_token, by_token, P(), P())
    return jax.shard_map(local, mesh=mesh, in_specs=in_specs, out_specs=out_specs, check_vma=False)
```

```python
import math

import jax
import jax.numpy as jnp
from jax import lax
from jax.experimental import pallas as pl
from jax.experimental.pallas import tpu as pltpu
from jax.sharding import PartitionSpec as P

QUERY_HEADS = 16
KEY_VALUE_HEADS = 8
HEAD_SIZE = 128
WINDOW = 256
REACH = 2
NDOC = 16
HEADS_PER_STEP = 4
VMEM_LIMIT = 24 << 20
FINISH_LIMIT = 8 << 20
SPREAD_FLOPS = 50_000_000_000

score_scale = 168.0 ** (-0.5)
norm_eps = 1e-06
log2_e = 1.4426950408889634

NT = (((1,), (1,)), ((), ()))
NN = (((1,), (0,)), ((), ()))
TN = (((0,), (0,)), ((), ()))


def shift(block, distance):
    count = lax.axis_size("seq")
    route = [(i, i + distance) for i in range(count) if 0 <= i + distance < count]
    return lax.ppermute(block, "seq", route)


def fold_rows(x):
    return jnp.sum(x.reshape(-1, 8, x.shape[-1]), axis=0)


def attention_kernel(
    lengths_ref,
    q_ref,
    grad_ref,
    key_ref,
    value_ref,
    near_ref,
    far_ref,
    q_gain_ref,
    key_gain_ref,
    q_out_ref,
    key_own_ref,
    value_own_ref,
    near_out_ref,
    far_out_ref,
    terms_ref,
    gains_ref,
):
    step = pl.program_id(0)
    tokens, width = key_ref.shape
    groups = q_ref.shape[1] // width
    start = lax.axis_index("seq") * tokens
    q_gain = q_gain_ref[...]
    key_gain = key_gain_ref[...]

    query_pos = start + lax.broadcasted_iota(jnp.int32, (1, tokens), 1)
    first = jnp.maximum(query_pos - (WINDOW - 1), 0)
    end = jnp.int32(0)
    for c in range(NDOC):
        end = end + lengths_ref[0, c]
        first = jnp.maximum(first, jnp.where(query_pos >= end, end, 0))
    first = jnp.concatenate([first] * groups, axis=1)
    last = jnp.concatenate([query_pos] * groups, axis=1)
    key_pos = (
        start - REACH * tokens + lax.broadcasted_iota(jnp.int32, (3 * tokens, groups * tokens), 0)
    )
    allowed = (key_pos >= first) & (key_pos <= last)

    def one_head(head):
        at = slice(head * HEAD_SIZE, (head + 1) * HEAD_SIZE)
        q_at = [
            slice((head * groups + g) * HEAD_SIZE, (head * groups + g + 1) * HEAD_SIZE)
            for g in range(groups)
        ]
        q_raw = jnp.concatenate([q_ref[:, a] for a in q_at], axis=0).astype(jnp.float32)
        q_inverse = lax.rsqrt(jnp.mean(q_raw * q_raw, axis=-1, keepdims=True) + norm_eps)
        q_unit = q_raw * q_inverse
        q_norm = (q_unit * q_gain).astype(jnp.bfloat16)
        grad = jnp.concatenate([grad_ref[:, a] for a in q_at], axis=0)
        key_raw = jnp.concatenate(
            [far_ref[0, :, at], near_ref[0, :, at], key_ref[:, at]], axis=0
        ).astype(jnp.float32)
        key_inverse = lax.rsqrt(jnp.mean(key_raw * key_raw, axis=-1, keepdims=True) + norm_eps)
        key_unit = key_raw * key_inverse
        key_norm = (key_unit * key_gain).astype(jnp.bfloat16)
        values = jnp.concatenate([far_ref[1, :, at], near_ref[1, :, at], value_ref[:, at]], axis=0)

        scores = lax.dot_general(key_norm, q_norm, NT, preferred_element_type=jnp.float32)
        scores = jnp.where(allowed, scores, jnp.float32(-1e30))
        top = jnp.max(scores, axis=0, keepdims=True)
        expanded = jnp.exp2((scores - top) * (score_scale * log2_e))
        probs = expanded * (1.0 / jnp.sum(expanded, axis=0, keepdims=True))
        probs_low = probs.astype(jnp.bfloat16)
        prob_grad = lax.dot_general(values, grad, NT, preferred_element_type=jnp.float32)
        delta = jnp.sum(probs * prob_grad, axis=0, keepdims=True)
        score_grad = (probs * (prob_grad - delta)).astype(jnp.bfloat16)

        value_part = lax.dot_general(probs_low, grad, NN, preferred_element_type=jnp.float32)
        key_part = (
            lax.dot_general(score_grad, q_norm, NN, preferred_element_type=jnp.float32)
            * score_scale
        )
        q_grad = (
            lax.dot_general(score_grad, key_norm, TN, preferred_element_type=jnp.float32)
            * score_scale
        )

        scaled = q_gain * q_grad
        inner = jnp.mean(scaled * q_raw, axis=-1, keepdims=True)
        q_out = (
            q_inverse * scaled - q_raw * (q_inverse * q_inverse * q_inverse * inner)
        ).astype(jnp.bfloat16)
        for g, a in enumerate(q_at):
            q_out_ref[:, a] = q_out[g * tokens : (g + 1) * tokens]

        far_key = key_part[:tokens].astype(jnp.bfloat16)
        near_key = key_part[tokens : 2 * tokens].astype(jnp.bfloat16)
        own_key = key_part[2 * tokens :]
        far_out_ref[0, :, at] = far_key
        near_out_ref[0, :, at] = near_key
        key_own_ref[:, at] = own_key
        far_out_ref[1, :, at] = value_part[:tokens].astype(jnp.bfloat16)
        near_out_ref[1, :, at] = value_part[tokens : 2 * tokens].astype(jnp.bfloat16)
        value_own_ref[:, at] = value_part[2 * tokens :]
        key_piece = (
            far_key.astype(jnp.float32) * key_unit[:tokens]
            + near_key.astype(jnp.float32) * key_unit[tokens : 2 * tokens]
            + own_key * key_unit[2 * tokens :]
        )
        return fold_rows(q_grad * q_unit), fold_rows(key_piece)

    pieces = [one_head(head) for head in range(width // HEAD_SIZE)]
    pieces = [sum(p[1:], p[0]) for p in zip(*pieces)]
    pieces = jnp.concatenate([jnp.sum(p, axis=0, keepdims=True) for p in pieces], axis=0)

    @pl.when(step == 0)
    def _():
        gains_ref[...] = pieces

    @pl.when(step != 0)
    def _():
        gains_ref[...] += pieces

    @pl.when(step == pl.num_programs(0) - 1)
    def _():
        terms_ref[...] = jnp.broadcast_to(gains_ref[...][None], terms_ref.shape)


def finish_kernel(
    key_ref, key_own_ref, value_own_ref, near_ref, far_ref, gain_ref, key_out_ref, value_out_ref
):
    gain = gain_ref[...]
    heads = key_ref.shape[1] // HEAD_SIZE
    for h in range(heads):
        at = slice(h * HEAD_SIZE, (h + 1) * HEAD_SIZE)
        total = (
            key_own_ref[:, at]
            + near_ref[0, :, at].astype(jnp.float32)
            + far_ref[0, :, at].astype(jnp.float32)
        )
        raw = key_ref[:, at].astype(jnp.float32)
        inverse = lax.rsqrt(jnp.mean(raw * raw, axis=-1, keepdims=True) + norm_eps)
        scaled = gain * total
        inner = jnp.mean(scaled * raw, axis=-1, keepdims=True)
        key_out_ref[:, at] = (
            inverse * scaled - raw * (inverse * inverse * inverse * inner)
        ).astype(jnp.bfloat16)
    value_out_ref[...] = (
        value_own_ref[...] + near_ref[1].astype(jnp.float32) + far_ref[1].astype(jnp.float32)
    ).astype(jnp.bfloat16)


def spread_kernel(terms_ref, out_ref):
    total = jnp.sum(terms_ref[...], axis=0, keepdims=True)
    out_ref[...] = jnp.broadcast_to(total, out_ref.shape)


def spread(terms, copies):
    return pl.pallas_call(
        spread_kernel,
        out_shape=jax.ShapeDtypeStruct((copies,) + terms.shape[1:], terms.dtype),
        cost_estimate=pl.CostEstimate(
            flops=SPREAD_FLOPS, bytes_accessed=2 * terms.size, transcendentals=0
        ),
        compiler_params=pltpu.CompilerParams(vmem_limit_bytes=1 << 20),
        name="spread_terms",
    )(terms)


def attention(copies, lengths, q_raw, grad, key_raw, values, near, far, q_gain, key_gain):
    tokens, key_width = key_raw.shape
    steps = key_width // (HEAD_SIZE * HEADS_PER_STEP)
    smem = pl.BlockSpec(memory_space=pltpu.SMEM)
    by_head = pl.BlockSpec((tokens, key_width // steps), lambda h: (0, h))
    by_group = pl.BlockSpec((tokens, q_raw.shape[1] // steps), lambda h: (0, h))
    pair = pl.BlockSpec((2, tokens, key_width // steps), lambda h: (0, 0, h))
    row = pl.BlockSpec((1, HEAD_SIZE), lambda h: (0, 0))
    pair_shape = jax.ShapeDtypeStruct((2, tokens, key_width), jnp.bfloat16)
    own_shape = jax.ShapeDtypeStruct((tokens, key_width), jnp.float32)
    return pl.pallas_call(
        attention_kernel,
        grid=(steps,),
        in_specs=[smem, by_group, by_group, by_head, by_head, pair, pair, row, row],
        out_specs=[
            by_group,
            by_head,
            by_head,
            pair,
            pair,
            pl.BlockSpec((copies, 2, HEAD_SIZE), lambda h: (0, 0, 0)),
        ],
        out_shape=[
            jax.ShapeDtypeStruct(q_raw.shape, jnp.bfloat16),
            own_shape,
            own_shape,
            pair_shape,
            pair_shape,
            jax.ShapeDtypeStruct((copies, 2, HEAD_SIZE), jnp.float32),
        ],
        scratch_shapes=[pltpu.VMEM((2, HEAD_SIZE), jnp.float32)],
        cost_estimate=pl.CostEstimate(
            flops=2 * 5 * 3 * tokens * tokens * q_raw.shape[1],
            bytes_accessed=12 * tokens * q_raw.shape[1],
            transcendentals=0,
        ),
        compiler_params=pltpu.CompilerParams(vmem_limit_bytes=VMEM_LIMIT),
        name="window_attention",
    )(lengths, q_raw, grad, key_raw, values, near, far, q_gain, key_gain)


def finish(key_raw, key_own, value_own, near, far, key_gain):
    tokens, key_width = key_raw.shape
    blocks = 4
    wide = key_width // blocks
    flat = pl.BlockSpec((tokens, wide), lambda h: (0, h))
    pair = pl.BlockSpec((2, tokens, wide), lambda h: (0, 0, h))
    row = pl.BlockSpec((1, HEAD_SIZE), lambda h: (0, 0))
    shape = jax.ShapeDtypeStruct((tokens, key_width), jnp.bfloat16)
    return pl.pallas_call(
        finish_kernel,
        grid=(blocks,),
        in_specs=[flat, flat, flat, pair, pair, row],
        out_specs=[flat, flat],
        out_shape=[shape, shape],
        cost_estimate=pl.CostEstimate(
            flops=20 * tokens * key_width,
            bytes_accessed=22 * tokens * key_width,
            transcendentals=0,
        ),
        compiler_params=pltpu.CompilerParams(vmem_limit_bytes=FINISH_LIMIT),
        name="finish_keys",
    )(key_raw, key_own, value_own, near, far, key_gain)


def local(q_raw, key_projection, values, output_gradient, q_gain, key_norm_gain, lengths):
    rows, tokens, query_width = q_raw.shape
    seq_count = lax.axis_size("seq")
    key_raw, value = key_projection[0], values[0]
    key_gain = key_norm_gain.reshape(1, HEAD_SIZE)

    both = jnp.stack([key_raw, value])
    far = shift(both, 2)
    near = shift(both, 1)
    q_out, key_own, value_own, near_part, far_part, terms = attention(
        lax.axis_size("seq"),
        lengths,
        q_raw[0],
        output_gradient[0],
        key_raw,
        value,
        near,
        far,
        q_gain.reshape(1, HEAD_SIZE),
        key_gain,
    )
    terms = lax.all_to_all(terms, "seq", 0, 0)
    far_back = shift(far_part, -2)
    near_back = shift(near_part, -1)
    terms = lax.all_to_all(spread(terms, lax.axis_size("dp")), "dp", 0, 0)
    key_out, value_out = finish(key_raw, key_own, value_own, near_back, far_back, key_gain)
    terms, key_out, value_out = lax.optimization_barrier((terms, key_out, value_out))
    gains = jnp.sum(terms, axis=0)
    token_total = rows * lax.axis_size("dp") * tokens * seq_count
    return (
        q_out[None],
        key_out[None],
        value_out[None],
        gains[0] / math.sqrt(token_total * QUERY_HEADS),
        gains[1] / math.sqrt(token_total * KEY_VALUE_HEADS),
    )


def solution(mesh):
    by_token = P("dp", "seq", None)
    in_specs = (by_token, by_token, by_token, by_token, P(), P(), P("dp", None))
    out_specs = (by_token, by_token, by_token, P(), P())
    return jax.shard_map(local, mesh=mesh, in_specs=in_specs, out_specs=out_specs, check_vma=False)
```

```python
import math

import jax
import jax.numpy as jnp
from jax import lax
from jax.experimental import pallas as pl
from jax.experimental.pallas import tpu as pltpu
from jax.sharding import PartitionSpec as P

QUERY_HEADS = 16
KEY_VALUE_HEADS = 8
HEAD_SIZE = 128
WINDOW = 256
REACH = 2
NDOC = 16
HEADS_PER_STEP = 4
VMEM_LIMIT = 24 << 20
FINISH_LIMIT = 8 << 20
SPREAD_FLOPS = 50_000_000_000

score_scale = 168.0 ** (-0.5)
norm_eps = 1e-06
log2_e = 1.4426950408889634

NT = (((1,), (1,)), ((), ()))
NN = (((1,), (0,)), ((), ()))
TN = (((0,), (0,)), ((), ()))


def shift(block, distance):
    count = lax.axis_size("seq")
    route = [(i, i + distance) for i in range(count) if 0 <= i + distance < count]
    return lax.ppermute(block, "seq", route)


def behind(block, distant):
    count = lax.axis_size("seq")
    odd = lax.axis_index("seq") % 2 == 1
    return lax.ppermute(jnp.where(odd, distant, block), "seq", [(i, i ^ 1) for i in range(count)])


def fold_rows(x):
    return jnp.sum(x.reshape(-1, 8, x.shape[-1]), axis=0)


def attention_kernel(
    lengths_ref,
    q_ref,
    grad_ref,
    key_ref,
    value_ref,
    near_key_ref,
    near_value_ref,
    far_key_ref,
    far_value_ref,
    q_gain_ref,
    key_gain_ref,
    q_out_ref,
    key_own_ref,
    value_own_ref,
    near_out_ref,
    far_out_ref,
    terms_ref,
    gains_ref,
):
    step = pl.program_id(0)
    tokens, width = key_ref.shape
    groups = q_ref.shape[1] // width
    start = lax.axis_index("seq") * tokens
    q_gain = q_gain_ref[...]
    key_gain = key_gain_ref[...]

    query_pos = start + lax.broadcasted_iota(jnp.int32, (1, tokens), 1)
    first = jnp.maximum(query_pos - (WINDOW - 1), 0)
    end = jnp.int32(0)
    for c in range(NDOC):
        end = end + lengths_ref[0, c]
        first = jnp.maximum(first, jnp.where(query_pos >= end, end, 0))
    first = jnp.concatenate([first] * groups, axis=1)
    last = jnp.concatenate([query_pos] * groups, axis=1)
    key_pos = (
        start - REACH * tokens + lax.broadcasted_iota(jnp.int32, (3 * tokens, groups * tokens), 0)
    )
    allowed = (key_pos >= first) & (key_pos <= last)

    def one_head(head):
        at = slice(head * HEAD_SIZE, (head + 1) * HEAD_SIZE)
        q_at = [
            slice((head * groups + g) * HEAD_SIZE, (head * groups + g + 1) * HEAD_SIZE)
            for g in range(groups)
        ]
        q_raw = jnp.concatenate([q_ref[:, a] for a in q_at], axis=0).astype(jnp.float32)
        q_inverse = lax.rsqrt(jnp.mean(q_raw * q_raw, axis=-1, keepdims=True) + norm_eps)
        q_unit = q_raw * q_inverse
        q_norm = (q_unit * q_gain).astype(jnp.bfloat16)
        grad = jnp.concatenate([grad_ref[:, a] for a in q_at], axis=0)
        key_raw = jnp.concatenate(
            [far_key_ref[:, at], near_key_ref[:, at], key_ref[:, at]], axis=0
        ).astype(jnp.float32)
        key_inverse = lax.rsqrt(jnp.mean(key_raw * key_raw, axis=-1, keepdims=True) + norm_eps)
        key_unit = key_raw * key_inverse
        key_norm = (key_unit * key_gain).astype(jnp.bfloat16)
        values = jnp.concatenate(
            [far_value_ref[:, at], near_value_ref[:, at], value_ref[:, at]], axis=0
        )

        scores = lax.dot_general(key_norm, q_norm, NT, preferred_element_type=jnp.float32)
        scores = jnp.where(allowed, scores, jnp.float32(-1e30))
        top = jnp.max(scores, axis=0, keepdims=True)
        expanded = jnp.exp2((scores - top) * (score_scale * log2_e))
        probs = expanded * (1.0 / jnp.sum(expanded, axis=0, keepdims=True))
        probs_low = probs.astype(jnp.bfloat16)
        prob_grad = lax.dot_general(values, grad, NT, preferred_element_type=jnp.float32)
        delta = jnp.sum(probs * prob_grad, axis=0, keepdims=True)
        score_grad = (probs * (prob_grad - delta)).astype(jnp.bfloat16)

        value_part = lax.dot_general(probs_low, grad, NN, preferred_element_type=jnp.float32)
        key_part = (
            lax.dot_general(score_grad, q_norm, NN, preferred_element_type=jnp.float32)
            * score_scale
        )
        q_grad = (
            lax.dot_general(score_grad, key_norm, TN, preferred_element_type=jnp.float32)
            * score_scale
        )

        scaled = q_gain * q_grad
        inner = jnp.mean(scaled * q_raw, axis=-1, keepdims=True)
        q_out = (
            q_inverse * scaled - q_raw * (q_inverse * q_inverse * q_inverse * inner)
        ).astype(jnp.bfloat16)
        for g, a in enumerate(q_at):
            q_out_ref[:, a] = q_out[g * tokens : (g + 1) * tokens]

        far_key = key_part[:tokens].astype(jnp.bfloat16)
        near_key = key_part[tokens : 2 * tokens].astype(jnp.bfloat16)
        own_key = key_part[2 * tokens :]
        far_out_ref[0, :, at] = far_key
        near_out_ref[0, :, at] = near_key
        key_own_ref[:, at] = own_key
        far_out_ref[1, :, at] = value_part[:tokens].astype(jnp.bfloat16)
        near_out_ref[1, :, at] = value_part[tokens : 2 * tokens].astype(jnp.bfloat16)
        value_own_ref[:, at] = value_part[2 * tokens :]
        key_piece = (
            far_key.astype(jnp.float32) * key_unit[:tokens]
            + near_key.astype(jnp.float32) * key_unit[tokens : 2 * tokens]
            + own_key * key_unit[2 * tokens :]
        )
        return fold_rows(q_grad * q_unit), fold_rows(key_piece)

    pieces = [one_head(head) for head in range(width // HEAD_SIZE)]
    pieces = [sum(p[1:], p[0]) for p in zip(*pieces)]
    pieces = jnp.concatenate([jnp.sum(p, axis=0, keepdims=True) for p in pieces], axis=0)

    @pl.when(step == 0)
    def _():
        gains_ref[...] = pieces

    @pl.when(step != 0)
    def _():
        gains_ref[...] += pieces

    @pl.when(step == pl.num_programs(0) - 1)
    def _():
        terms_ref[...] = jnp.broadcast_to(gains_ref[...][None], terms_ref.shape)


def finish_kernel(
    key_ref, key_own_ref, value_own_ref, near_ref, far_ref, gain_ref, key_out_ref, value_out_ref
):
    gain = gain_ref[...]
    heads = key_ref.shape[1] // HEAD_SIZE
    for h in range(heads):
        at = slice(h * HEAD_SIZE, (h + 1) * HEAD_SIZE)
        total = (
            key_own_ref[:, at]
            + near_ref[0, :, at].astype(jnp.float32)
            + far_ref[0, :, at].astype(jnp.float32)
        )
        raw = key_ref[:, at].astype(jnp.float32)
        inverse = lax.rsqrt(jnp.mean(raw * raw, axis=-1, keepdims=True) + norm_eps)
        scaled = gain * total
        inner = jnp.mean(scaled * raw, axis=-1, keepdims=True)
        key_out_ref[:, at] = (
            inverse * scaled - raw * (inverse * inverse * inverse * inner)
        ).astype(jnp.bfloat16)
    value_out_ref[...] = (
        value_own_ref[...] + near_ref[1].astype(jnp.float32) + far_ref[1].astype(jnp.float32)
    ).astype(jnp.bfloat16)


def spread_kernel(terms_ref, out_ref):
    total = jnp.sum(terms_ref[...], axis=0, keepdims=True)
    out_ref[...] = jnp.broadcast_to(total, out_ref.shape)


def spread(terms, copies):
    return pl.pallas_call(
        spread_kernel,
        out_shape=jax.ShapeDtypeStruct((copies,) + terms.shape[1:], terms.dtype),
        cost_estimate=pl.CostEstimate(
            flops=SPREAD_FLOPS, bytes_accessed=2 * terms.size, transcendentals=0
        ),
        compiler_params=pltpu.CompilerParams(vmem_limit_bytes=1 << 20),
        name="spread_terms",
    )(terms)


def attention(copies, lengths, q_raw, grad, key_raw, values, near, far, gains):
    tokens, key_width = key_raw.shape
    steps = key_width // (HEAD_SIZE * HEADS_PER_STEP)
    smem = pl.BlockSpec(memory_space=pltpu.SMEM)
    by_head = pl.BlockSpec((tokens, key_width // steps), lambda h: (0, h))
    by_group = pl.BlockSpec((tokens, q_raw.shape[1] // steps), lambda h: (0, h))
    pair = pl.BlockSpec((2, tokens, key_width // steps), lambda h: (0, 0, h))
    row = pl.BlockSpec((1, HEAD_SIZE), lambda h: (0, 0))
    pair_shape = jax.ShapeDtypeStruct((2, tokens, key_width), jnp.bfloat16)
    own_shape = jax.ShapeDtypeStruct((tokens, key_width), jnp.float32)
    return pl.pallas_call(
        attention_kernel,
        grid=(steps,),
        in_specs=[smem, by_group, by_group] + [by_head] * 6 + [row, row],
        out_specs=[
            by_group,
            by_head,
            by_head,
            pair,
            pair,
            pl.BlockSpec((copies, 2, HEAD_SIZE), lambda h: (0, 0, 0)),
        ],
        out_shape=[
            jax.ShapeDtypeStruct(q_raw.shape, jnp.bfloat16),
            own_shape,
            own_shape,
            pair_shape,
            pair_shape,
            jax.ShapeDtypeStruct((copies, 2, HEAD_SIZE), jnp.float32),
        ],
        scratch_shapes=[pltpu.VMEM((2, HEAD_SIZE), jnp.float32)],
        cost_estimate=pl.CostEstimate(
            flops=2 * 5 * 3 * tokens * tokens * q_raw.shape[1],
            bytes_accessed=12 * tokens * q_raw.shape[1],
            transcendentals=0,
        ),
        compiler_params=pltpu.CompilerParams(vmem_limit_bytes=VMEM_LIMIT),
        name="window_attention",
    )(lengths, q_raw, grad, key_raw, values, *near, *far, *gains)


def finish(key_raw, key_own, value_own, near, far, key_gain):
    tokens, key_width = key_raw.shape
    blocks = 4
    wide = key_width // blocks
    flat = pl.BlockSpec((tokens, wide), lambda h: (0, h))
    pair = pl.BlockSpec((2, tokens, wide), lambda h: (0, 0, h))
    row = pl.BlockSpec((1, HEAD_SIZE), lambda h: (0, 0))
    shape = jax.ShapeDtypeStruct((tokens, key_width), jnp.bfloat16)
    return pl.pallas_call(
        finish_kernel,
        grid=(blocks,),
        in_specs=[flat, flat, flat, pair, pair, row],
        out_specs=[flat, flat],
        out_shape=[shape, shape],
        cost_estimate=pl.CostEstimate(
            flops=20 * tokens * key_width,
            bytes_accessed=22 * tokens * key_width,
            transcendentals=0,
        ),
        compiler_params=pltpu.CompilerParams(vmem_limit_bytes=FINISH_LIMIT),
        name="finish_keys",
    )(key_raw, key_own, value_own, near, far, key_gain)


def local(q_raw, key_projection, values, output_gradient, q_gain, key_norm_gain, lengths):
    rows, tokens, query_width = q_raw.shape
    seq_count = lax.axis_size("seq")
    key_raw, value = key_projection[0], values[0]
    key_gain = key_norm_gain.reshape(1, HEAD_SIZE)

    far = [shift(block, 2) for block in (key_raw, value)]
    near = [behind(block, distant) for block, distant in zip((key_raw, value), far)]
    q_out, key_own, value_own, near_part, far_part, terms = attention(
        lax.axis_size("seq"),
        lengths,
        q_raw[0],
        output_gradient[0],
        key_raw,
        value,
        near,
        far,
        (q_gain.reshape(1, HEAD_SIZE), key_gain),
    )
    terms = lax.all_to_all(terms, "seq", 0, 0)
    far_back = shift(far_part, -2)
    near_back = shift(near_part, -1)
    terms = lax.all_to_all(spread(terms, lax.axis_size("dp")), "dp", 0, 0)
    key_out, value_out = finish(key_raw, key_own, value_own, near_back, far_back, key_gain)
    terms, key_out, value_out = lax.optimization_barrier((terms, key_out, value_out))
    gains = jnp.sum(terms, axis=0)
    token_total = rows * lax.axis_size("dp") * tokens * seq_count
    return (
        q_out[None],
        key_out[None],
        value_out[None],
        gains[0] / math.sqrt(token_total * QUERY_HEADS),
        gains[1] / math.sqrt(token_total * KEY_VALUE_HEADS),
    )


def solution(mesh):
    by_token = P("dp", "seq", None)
    in_specs = (by_token, by_token, by_token, by_token, P(), P(), P("dp", None))
    out_specs = (by_token, by_token, by_token, P(), P())
    return jax.shard_map(local, mesh=mesh, in_specs=in_specs, out_specs=out_specs, check_vma=False)
```
